256 devices in a mesh: col: 4 (over z_lo, core), dp: 64 (over y, x, z_hi).
Axes of the slice: x: 4, y: 4, z: 8 (z_hi: 4, z_lo: 2; z = z_hi * 2 + z_lo), core: 2. Of those that a mesh axis runs over, the one named last changes fastest.
Arguments:
- layer_input: bfloat16 [8192, 8192], P('dp', 'col'), may hold values from -6 to 6
- query_cotangent: bfloat16 [8192, 4096], P('dp'), may hold values from -0.06591797 to 0.06591797
- key_cotangent: bfloat16 [8192, 1024], P('dp'), may hold values from -0.06591797 to 0.06591797
- up_cotangent: bfloat16 [8192, 14336], P('dp'), may hold values from -0.06591797 to 0.06591797
- query_weight: bfloat16 [4096, 8192], P('dp', 'col'), may hold values from -24 to 24
- key_weight: bfloat16 [1024, 8192], P('dp', 'col'), may hold values from -24 to 24
- up_weight: bfloat16 [14336, 8192], P('dp', 'col'), may hold values from -24 to 24
- moment_query: bfloat16 [4096, 8192], P('dp', 'col'), may hold values from -3 to 3
- moment_key: bfloat16 [1024, 8192], P('dp', 'col'), may hold values from -3 to 3
- moment_up: bfloat16 [14336, 8192], P('dp', 'col'), may hold values from -3 to 3
- second_query: bfloat16 [4096, 8192], P('dp', 'col'), may hold values from 0.25 to 4
- second_key: bfloat16 [1024, 8192], P('dp', 'col'), may hold values from 0.25 to 4
- second_up: bfloat16 [14336, 8192], P('dp', 'col'), may hold values from 0.25 to 4
Outputs:
- updated_query: bfloat16 [4096, 8192], P('dp', 'col')
- updated_key: bfloat16 [1024, 8192], P('dp', 'col')
- updated_up: bfloat16 [14336, 8192], P('dp', 'col')
- mean_query: bfloat16 [4096, 8192], P('dp', 'col')
- mean_key: bfloat16 [1024, 8192], P('dp', 'col')
- mean_up: bfloat16 [14336, 8192], P('dp', 'col')
- square_query: bfloat16 [4096, 8192], P('dp', 'col')
- square_key: bfloat16 [1024, 8192], P('dp', 'col')
- square_up: bfloat16 [14336, 8192], P('dp', 'col')
The draws below stay inside these ranges and needn't reach their ends.
All inputs are finite; a program needn't handle non-finite values.
Results may differ from the reference program's by a relative error of at most 0.001.
Values may be sent and summed in bfloat16 or wider, within the bound.
A program may use at most 128 MiB of HBM per device.

```python
import math
import jax
import jax.numpy as jnp
from jax import lax

D = 8192
FF_WIN = 14336
QROWS = 4096
KROWS = 1024
TOKENS = 8192


def scaled_weight(key, rows, which):
    key = jax.random.fold_in(key, which)
    key_base = jax.random.fold_in(key, 11)
    key_cols = jax.random.fold_in(key, 12)
    key_blocks = jax.random.fold_in(key, 13)
    key_rows = jax.random.fold_in(key, 14)
    base = jnp.clip(jax.random.normal(key_base, (rows, D), jnp.float32), -4.0, 4.0)
    column_scale = jnp.exp(jax.random.uniform(key_cols, (1, D), jnp.float32, math.log(0.25), math.log(2.5)))
    block_scale = jnp.exp(jax.random.uniform(key_blocks, (32,), jnp.float32, math.log(0.5), math.log(1.5)))
    block_scale = jnp.repeat(block_scale, D // 32).reshape(1, D)
    row_scale = jnp.exp(jax.random.uniform(key_rows, (rows, 1), jnp.float32, math.log(0.4), math.log(1.6)))
    return (base * column_scale * block_scale * row_scale).astype(jnp.bfloat16)


def draw_query_weight(key, part):
    return scaled_weight(key, QROWS, 101)


def draw_key_weight(key, part):
    return scaled_weight(key, KROWS, 202)


def draw_up_weight(key, part):
    return scaled_weight(key, FF_WIN, 303)


def level_of(own_key, extent, shards, smallest, largest):
    def one(axis_at, shards_of):
        draws = jax.random.uniform(jax.random.fold_in(jax.random.fold_in(own_key, 6), axis_at), (shards_of,), jnp.float32, smallest / len(shards), largest / len(shards))
        return jnp.repeat(jnp.exp(draws), extent[axis_at] // shards_of).reshape((-1,) + (1,) * (len(extent) - axis_at - 1))

    factor_of = one(*shards[0])
    for cut in shards[1:]:
        factor_of = factor_of * one(*cut)
    return factor_of


def scatter_about(rng, extent, width, bound, cuts=(), held_as=jnp.bfloat16):
    drawn = width * jax.random.normal(rng, extent, jnp.float32)
    if cuts:
        drawn = drawn * level_of(rng, extent, cuts, -0.22, 0.18)
    return jnp.clip(drawn, -bound, bound).astype(held_as)


def setup_inputs(seed: int = 0) -> dict:
    keys = jax.random.split(jax.random.key(seed), 14)
    return {
        "layer_input": scatter_about(keys[0], (TOKENS, D), 1.0, 6.0, ((0, 64), (1, 4))),
        "query_cotangent": scatter_about(keys[1], (TOKENS, QROWS), (1.0 / TOKENS ** 0.5), 0.06591797, ((0, 64),)),
        "key_cotangent": scatter_about(keys[2], (TOKENS, KROWS), (1.0 / TOKENS ** 0.5), 0.06591797, ((0, 64),)),
        "up_cotangent": scatter_about(keys[3], (TOKENS, FF_WIN), (1.0 / TOKENS ** 0.5), 0.06591797, ((0, 64),)),
        "query_weight": draw_query_weight(jax.random.fold_in(keys[13], 71), 0),
        "key_weight": draw_key_weight(jax.random.fold_in(keys[13], 71), 0),
        "up_weight": draw_up_weight(jax.random.fold_in(keys[13], 71), 0),
        "moment_query": scatter_about(keys[7], (QROWS, D), 0.5, 3.0, ((0, 64), (1, 4))),
        "moment_key": scatter_about(keys[8], (KROWS, D), 0.5, 3.0, ((0, 64), (1, 4))),
        "moment_up": scatter_about(keys[9], (FF_WIN, D), 0.5, 3.0, ((0, 64), (1, 4))),
        "second_query": jnp.clip(jnp.exp(math.log(4.0) - 2.7725887 * jax.random.uniform(keys[10], (QROWS, D), jnp.float32) ** level_of(keys[10], (QROWS, D), ((0, 64), (1, 4)), -0.2, 0.2)), 0.25, 4.0).astype(jnp.bfloat16),
        "second_key": jnp.clip(jnp.exp(math.log(4.0) - 2.7725887 * jax.random.uniform(keys[11], (KROWS, D), jnp.float32) ** level_of(keys[11], (KROWS, D), ((0, 64), (1, 4)), -0.2, 0.2)), 0.25, 4.0).astype(jnp.bfloat16),
        "second_up": jnp.clip(jnp.exp(math.log(4.0) - 2.7725887 * jax.random.uniform(keys[12], (FF_WIN, D), jnp.float32) ** level_of(keys[12], (FF_WIN, D), ((0, 64), (1, 4)), -0.2, 0.2)), 0.25, 4.0).astype(jnp.bfloat16),
    }


beta_one = 0.9
beta_two = 0.95
rate = 0.1
eps_adam = 1e-08
eps_norm = 1e-06

def update(cotangent, inputs, weight, moment, second):
    gradient = jnp.dot(cotangent.T, inputs, preferred_element_type=jnp.float32)
    first = beta_one * moment.astype(jnp.float32) + (1.0 - beta_one) * gradient
    square = beta_two * second.astype(jnp.float32) + (1.0 - beta_two) * gradient * gradient
    step = weight.astype(jnp.float32) - rate * first / (jnp.sqrt(square) + eps_adam)
    power = lax.optimization_barrier(jnp.mean(step * step, axis=1, keepdims=True))
    updated = (step / jnp.sqrt(power + eps_norm)).astype(jnp.bfloat16)
    return (updated, first.astype(jnp.bfloat16), square.astype(jnp.bfloat16))

def reference(layer_input, query_cotangent, key_cotangent, up_cotangent, query_weight, key_weight, up_weight, moment_query, moment_key, moment_up, second_query, second_key, second_up):
    new_query, first_query, sq_query = update(query_cotangent, layer_input, query_weight, moment_query, second_query)
    new_key, first_key, sq_key = update(key_cotangent, layer_input, key_weight, moment_key, second_key)
    new_up, first_up, sq_up = update(up_cotangent, layer_input, up_weight, moment_up, second_up)
    return (new_query, new_key, new_up, first_query, first_key, first_up, sq_query, sq_key, sq_up)
```

```python
import functools

import jax
import jax.numpy as jnp
from jax import lax
from jax.experimental import pallas as pl
from jax.experimental.pallas import tpu as pltpu
from jax.sharding import PartitionSpec as P

beta_one = 0.9
beta_two = 0.95
rate = 0.1
eps_adam = 1e-08
eps_norm = 1e-06

MESH = pl.DeviceIdType.MESH
CHUNKS = 8
LANES = 128


def place():
    dp = lax.axis_index("dp")
    col = lax.axis_index("col")
    return dp // 16, lax.rem(dp // 4, 4), lax.rem(dp, 4), col // 2, lax.rem(col, 2)


def wrap(v):
    return lax.rem(v + 8, 4)


def exchange_kernel(
    ct_ref, x_ref, g_ref, c_buf, x_buf, p_buf, r_buf, ssem, rsem, lsem
):
    y, x, z, lo, core = place()
    toward = 2 * lo - 1
    rows = g_ref.shape[0]
    half = 2 * rows
    width = x_ref.shape[1] // CHUNKS

    def device(dy=0, dx=0, dz=0, flip_lo=False, flip_core=False):
        lo_to = 1 - lo if flip_lo else lo
        core_to = 1 - core if flip_core else core
        return {
            "dp": wrap(y + dy) * 16 + wrap(x + dx) * 4 + wrap(z + dz),
            "col": lo_to * 2 + core_to,
        }

    peers = [device(dy=d) for d in (1, 2, 3)]
    peers += [device(dz=d) for d in (1, 2, 3)]
    peers += [device(dx=d) for d in (1, 3)]
    peers += [device(dy=d, dz=toward, flip_lo=True) for d in range(4)]
    peers += [device(dy=d, dz=2, flip_lo=True) for d in range(4)]
    peers += [device(flip_lo=True), device(flip_core=True)]
    barrier = pltpu.get_barrier_semaphore()
    for peer in peers:
        pl.semaphore_signal(barrier, inc=1, device_id=peer, device_id_type=MESH)
    pl.semaphore_wait(barrier, len(peers))

    used = [0]
    pending = []

    def remote(src, dst, to):
        k = used[0]
        used[0] += 1
        return pltpu.make_async_remote_copy(
            src_ref=src,
            dst_ref=dst,
            send_sem=ssem.at[k],
            recv_sem=rsem.at[k],
            device_id=to,
            device_id_type=MESH,
        )

    def go(copy):
        copy.start()
        pending.append(copy)
        return copy

    def c_slot(slot):
        lanes = pl.ds(pl.multiple_of(slot * LANES, LANES), LANES)
        return c_buf.at[pl.ds(pl.multiple_of(core * half, 16), half), lanes]

    def ct_piece(dy, dz):
        return ct_ref.at[wrap(y + dy) * 4 + wrap(z + dz)]

    def send_c(slot, dy, dz, flip):
        return go(remote(ct_piece(dy, dz), c_slot(slot), device(dy=dy, dz=dz, flip_lo=flip)))

    def cols(j):
        return pl.ds(j * width, width)

    order = (0, 1, 3, 2)
    side = wrap(-toward)
    facing = [send_c(wrap(-dy) * 4 + side, dy, toward, True) for dy in order]
    far = [send_c(wrap(-(lo + 2 * i)) * 4 + 2, lo + 2 * i, 2, True) for i in range(2)]
    near = [send_c(((-dy) % 4) * 4, dy, 0, False) for dy in (1, 3, 2)]
    own_c = pltpu.make_async_copy(ct_piece(0, 0), c_slot(0), lsem.at[0])
    own_c.start()
    own_x = pltpu.make_async_copy(x_ref, x_buf.at[pl.ds(0, LANES)], lsem.at[1])
    own_x.start()
    own_up = go(remote(x_ref, x_buf.at[pl.ds(12 * LANES, LANES)], device(dy=1)))
    own_down = go(remote(x_ref, x_buf.at[pl.ds(4 * LANES, LANES)], device(dy=3)))
    along_z = []
    for j in range(CHUNKS):
        along_z.append(
            [
                go(
                    remote(
                        x_ref.at[:, cols(j)],
                        x_buf.at[pl.ds(((-dz) % 4) * LANES, LANES), cols(j)],
                        device(dz=dz),
                    )
                )
                for dz in (1, 3, 2)
            ]
        )

    def share(slot):
        place_at = c_slot(slot)
        return go(remote(place_at, place_at, device(flip_core=True)))

    def pass_on(slot):
        place_at = c_slot(slot)
        return go(remote(place_at, place_at, device(flip_lo=True)))

    shared = []
    own_c.wait()
    shared.append(share(0))
    for copy, dy in zip(near, (1, 3, 2)):
        copy.wait_recv()
        shared.append(share(((-dy) % 4) * 4))
    passed = []
    mine = wrap(toward)
    for copy, dy in zip(facing, order):
        copy.wait_recv()
        slot = wrap(-dy) * 4 + mine
        passed.append(pass_on(slot))
        shared.append(share(slot))
    for i, copy in enumerate(far):
        copy.wait_recv()
        slot = wrap(-((1 - lo) + 2 * i)) * 4 + 2
        passed.append(pass_on(slot))
        shared.append(share(slot))
    own_up.wait_recv()
    own_fwd = go(
        remote(
            x_buf.at[pl.ds(12 * LANES, LANES)],
            x_buf.at[pl.ds(8 * LANES, LANES)],
            device(dy=1),
        )
    )

    up, down, fwd_up, fwd_down = {}, {}, {}, {}

    def stage_y(j):
        for copy in along_z[j]:
            copy.wait_recv()
        src = x_buf.at[pl.ds(LANES, 3 * LANES), cols(j)]
        up[j] = go(remote(src, x_buf.at[pl.ds(13 * LANES, 3 * LANES), cols(j)], device(dy=1)))
        down[j] = go(remote(src, x_buf.at[pl.ds(5 * LANES, 3 * LANES), cols(j)], device(dy=3)))

    def stage_forward(j):
        up[j].wait_recv()
        fwd_up[j] = go(
            remote(
                x_buf.at[pl.ds(13 * LANES, LANES), cols(j)],
                x_buf.at[pl.ds(9 * LANES, LANES), cols(j)],
                device(dy=1),
            )
        )
        down[j].wait_recv()
        fwd_down[j] = go(
            remote(
                x_buf.at[pl.ds(6 * LANES, 2 * LANES), cols(j)],
                x_buf.at[pl.ds(10 * LANES, 2 * LANES), cols(j)],
                device(dy=3),
            )
        )

    ring = {}

    def ring_send(j, step):
        for way, sign in ((0, 1), (1, -1)):
            target = wrap(x - sign * (step + 1))
            if step > 0:
                ring[j, step - 1, way].wait_recv()
                p_buf[j, target, way] = p_buf[j, target, way] + r_buf[j, step - 1, way]
            ring[j, step, way] = go(
                remote(p_buf.at[j, target, way], r_buf.at[j, step, way], device(dx=sign))
            )

    def finish(j):
        for way in (0, 1):
            ring[j, 2, way].wait_recv()
            at = pl.ds(j * width + way * (width // 2), width // 2)
            g_ref[:, at] = p_buf[j, x, way] + r_buf[j, 2, way]

    def multiply(j):
        fwd_up[j].wait_recv()
        fwd_down[j].wait_recv()

        def one(d, carry):
            lhs = c_buf[pl.ds(pl.multiple_of(d * rows, 16), rows), :]
            out = jnp.dot(lhs, x_buf[:, cols(j)], preferred_element_type=jnp.float32)
            p_buf[j, d, 0] = out[:, : width // 2]
            p_buf[j, d, 1] = out[:, width // 2 :]
            return carry

        lax.fori_loop(0, 4, one, 0)

    stage_y(0)
    other = wrap(-toward)
    for copy, dy in zip(passed[:4], order):
        copy.wait_recv()
        shared.append(share(wrap(-dy) * 4 + other))
    for i, copy in enumerate(passed[4:]):
        copy.wait_recv()
        shared.append(share(wrap(-(lo + 2 * i)) * 4 + 2))
    stage_y(1)
    stage_forward(0)
    own_x.wait()
    own_down.wait_recv()
    own_fwd.wait_recv()
    for copy in shared:
        copy.wait_recv()

    for j in range(CHUNKS + 3):
        if j + 2 < CHUNKS:
            stage_y(j + 2)
        if j + 1 < CHUNKS:
            stage_forward(j + 1)
        if j < CHUNKS:
            multiply(j)
            ring_send(j, 0)
        if 0 <= j - 1 < CHUNKS:
            ring_send(j - 1, 1)
        if 0 <= j - 2 < CHUNKS:
            ring_send(j - 2, 2)
        if 0 <= j - 3 < CHUNKS:
            finish(j - 3)
    for copy in pending:
        copy.wait_send()


def gradient_of(ct, layer_input, rows):
    tokens, width = layer_input.shape
    chunk = width // CHUNKS
    count = 9 + 6 + 16 + 3 + CHUNKS * (3 + 4 + 6)
    return pl.pallas_call(
        exchange_kernel,
        out_shape=jax.ShapeDtypeStruct((rows, width), jnp.float32),
        in_specs=[pl.BlockSpec(memory_space=pl.ANY)] * 2,
        out_specs=pl.BlockSpec(memory_space=pltpu.VMEM),
        scratch_shapes=[
            pltpu.VMEM((4 * rows, 16 * tokens), jnp.bfloat16),
            pltpu.VMEM((16 * tokens, width), jnp.bfloat16),
            pltpu.VMEM((CHUNKS, 4, 2, rows, chunk // 2), jnp.float32),
            pltpu.VMEM((CHUNKS, 3, 2, rows, chunk // 2), jnp.float32),
            pltpu.SemaphoreType.DMA((count,)),
            pltpu.SemaphoreType.DMA((count,)),
            pltpu.SemaphoreType.DMA((2,)),
        ],
        compiler_params=pltpu.CompilerParams(
            collective_id=0, has_side_effects=True, vmem_limit_bytes=60 << 20
        ),
        name="exchange",
    )(ct, layer_input)


def optimizer_pass(gradient, weight, moment, second):
    first = beta_one * moment.astype(jnp.float32) + (1.0 - beta_one) * gradient
    square = beta_two * second.astype(jnp.float32) + (1.0 - beta_two) * gradient * gradient
    step = weight.astype(jnp.float32) - rate * first / (jnp.sqrt(square) + eps_adam)
    partial_power = jnp.sum(step * step, axis=1)
    return (step, first.astype(jnp.bfloat16), square.astype(jnp.bfloat16), partial_power)


def finish_rows(step, total_power, width):
    scale = jnp.sqrt(total_power / width + eps_norm)
    return (step / scale[:, None]).astype(jnp.bfloat16)


def per_device(
    layer_input,
    query_cotangent,
    key_cotangent,
    up_cotangent,
    query_weight,
    key_weight,
    up_weight,
    moment_query,
    moment_key,
    moment_up,
    second_query,
    second_key,
    second_up,
):
    tokens = layer_input.shape[0]
    query_rows = query_weight.shape[0]
    key_rows = key_weight.shape[0]
    up_rows = up_weight.shape[0]
    all_rows = query_rows + key_rows + up_rows
    width = layer_input.shape[1] * lax.axis_size("col")
    core = lax.rem(lax.axis_index("col"), 2)

    def halved(cotangent, rows):
        parts = cotangent.reshape(tokens, 4, 2, 2, 4, rows)
        return lax.dynamic_index_in_dim(parts, core, axis=2, keepdims=False)

    joined = jnp.concatenate(
        [
            halved(query_cotangent, query_rows),
            halved(key_cotangent, key_rows),
            halved(up_cotangent, up_rows),
        ],
        axis=4,
    )
    ct = joined.transpose(1, 3, 2, 4, 0).reshape(16, 2 * all_rows, tokens)
    gradient = gradient_of(ct, layer_input, all_rows)
    grad_query = gradient[:query_rows]
    grad_key = gradient[query_rows : query_rows + key_rows]
    grad_up = gradient[query_rows + key_rows :]
    step_query, first_query, sq_query, power_query = optimizer_pass(
        grad_query, query_weight, moment_query, second_query
    )
    step_key, first_key, sq_key, power_key = optimizer_pass(
        grad_key, key_weight, moment_key, second_key
    )
    step_up, first_up, sq_up, power_up = optimizer_pass(grad_up, up_weight, moment_up, second_up)
    total_query, total_key, total_up = lax.psum((power_query, power_key, power_up), "col")
    new_query = finish_rows(step_query, total_query, width)
    new_key = finish_rows(step_key, total_key, width)
    new_up = finish_rows(step_up, total_up, width)
    return (new_query, new_key, new_up, first_query, first_key, first_up, sq_query, sq_key, sq_up)


def solution(mesh):
    spread = P("dp", "col")
    return jax.shard_map(
        per_device,
        mesh=mesh,
        in_specs=(spread,) + (P("dp", None),) * 3 + (spread,) * 9,
        out_specs=(spread,) * 9,
        check_vma=False,
    )
```

```python
import functools

import jax
import jax.numpy as jnp
from jax import lax
from jax.experimental import pallas as pl
from jax.experimental.pallas import tpu as pltpu
from jax.sharding import PartitionSpec as P

beta_one = 0.9
beta_two = 0.95
rate = 0.1
eps_adam = 1e-08
eps_norm = 1e-06

MESH = pl.DeviceIdType.MESH
CHUNKS = 8
LANES = 128


def place():
    dp = lax.axis_index("dp")
    col = lax.axis_index("col")
    return dp // 16, lax.rem(dp // 4, 4), lax.rem(dp, 4), col // 2, lax.rem(col, 2)


def wrap(v):
    return lax.rem(v + 8, 4)


def exchange_kernel(
    x_ref,
    q_ref,
    k_ref,
    u_ref,
    wq_ref,
    wk_ref,
    wu_ref,
    mq_ref,
    mk_ref,
    mu_ref,
    vq_ref,
    vk_ref,
    vu_ref,
    step_ref,
    mean_ref,
    square_ref,
    power_ref,
    stage,
    kt_buf,
    ct_ref,
    opt_buf,
    c_buf,
    x_buf,
    p_buf,
    r_buf,
    lane_power,
    power_in,
    ssem,
    rsem,
    lsem,
):
    y, x, z, lo, core = place()
    rows_of = (wq_ref.shape[0], wk_ref.shape[0], wu_ref.shape[0])
    starts = (0, rows_of[0], rows_of[0] + rows_of[1])
    local = []

    def fetch(src, dst):
        copy = pltpu.make_async_copy(src, dst, lsem.at[len(local)])
        local.append(copy)
        copy.start()
        return copy

    staged = []
    for yy in range(4):
        for ref, n, at in zip((q_ref, k_ref, u_ref), rows_of, starts):
            span = 8 * n
            src = ref.at[:, pl.ds(pl.multiple_of((2 * yy + core) * span, LANES), span)]
            staged.append(fetch(src, stage.at[yy, :, pl.ds(8 * at, span)]))
    toward = 2 * lo - 1
    rows = step_ref.shape[0]
    width = x_ref.shape[1] // CHUNKS

    def device(dy=0, dx=0, dz=0, flip_lo=False, flip_core=False):
        lo_to = 1 - lo if flip_lo else lo
        core_to = 1 - core if flip_core else core
        return {
            "dp": wrap(y + dy) * 16 + wrap(x + dx) * 4 + wrap(z + dz),
            "col": lo_to * 2 + core_to,
        }

    peers = [device(dy=d) for d in (1, 2, 3)]
    peers += [device(dz=d) for d in (1, 2, 3)]
    peers += [device(dx=d) for d in (1, 3)]
    peers += [device(dy=d, dz=toward, flip_lo=True) for d in range(4)]
    peers += [device(dy=d, dz=2, flip_lo=True) for d in range(4)]
    peers += [device(flip_lo=True), device(flip_core=True)]
    peers += [device(flip_lo=True, flip_core=True)]
    barrier = pltpu.get_barrier_semaphore()
    for peer in peers:
        pl.semaphore_signal(barrier, inc=1, device_id=peer, device_id_type=MESH)
    pl.semaphore_wait(barrier, len(peers))

    used = [0]
    pending = []

    def remote(src, dst, to):
        k = used[0]
        used[0] += 1
        return pltpu.make_async_remote_copy(
            src_ref=src,
            dst_ref=dst,
            send_sem=ssem.at[k],
            recv_sem=rsem.at[k],
            device_id=to,
            device_id_type=MESH,
        )

    def go(copy):
        copy.start()
        pending.append(copy)
        return copy

    odd = lax.rem(x, 2)
    inner = (1 - odd, odd)

    def c_block(part, slot):
        return c_buf.at[slot, 2 * core + inner[part]]

    def ct_piece(part, dy, dz):
        return ct_ref.at[wrap(y + dy) * 4 + wrap(z + dz), part]

    def send_c(part, slot, dy, dz, flip):
        to = device(dy=dy, dz=dz, flip_lo=flip)
        return go(remote(ct_piece(part, dy, dz), c_block(part, slot), to))

    def cols(j):
        return pl.ds(j * width, width)

    order = (0, 1, 3, 2)
    side = wrap(-toward)
    mine = wrap(toward)
    facing, far, near, passed, shared = {}, {}, {}, {}, {}

    def c_sends(part):
        facing[part] = [
            send_c(part, wrap(-dy) * 4 + side, dy, toward, True) for dy in order
        ]
        far[part] = [
            send_c(part, wrap(-(lo + 2 * i)) * 4 + 2, lo + 2 * i, 2, True) for i in range(2)
        ]
        near[part] = [send_c(part, ((-dy) % 4) * 4, dy, 0, False) for dy in (1, 3, 2)]

    def z_sends(j):
        return [
            go(
                remote(
                    x_ref.at[:, cols(j)],
                    x_buf.at[pl.ds(((-dz) % 4) * LANES, LANES), cols(j)],
                    device(dz=dz),
                )
            )
            for dz in (1, 3, 2)
        ]

    own_up, own_down, own_fwd = {}, {}, {}

    def halves(h):
        return pl.ds(h * (x_ref.shape[1] // 2), x_ref.shape[1] // 2)

    def own_sends(h):
        at = halves(h)
        src = x_ref.at[:, at]
        own_up[h] = go(remote(src, x_buf.at[pl.ds(12 * LANES, LANES), at], device(dy=1)))
        own_down[h] = go(remote(src, x_buf.at[pl.ds(4 * LANES, LANES), at], device(dy=3)))

    def own_forward(h):
        own_up[h].wait_recv()
        src = x_buf.at[pl.ds(12 * LANES, LANES), halves(h)]
        own_fwd[h] = go(
            remote(src, x_buf.at[pl.ds(8 * LANES, LANES), halves(h)], device(dy=1))
        )

    def own_arrived(h):
        own_down[h].wait_recv()
        own_fwd[h].wait_recv()

    def turn(part):
        xl = inner[part]

        def one(yy, carry):
            if part == 0:
                kt_buf[yy] = stage[yy, :, 8 * starts[1] : 8 * starts[2]].T
            q_span, u_span = 4 * rows_of[0], 4 * rows_of[2]
            q_at = pl.multiple_of(xl * q_span, LANES)
            u_at = pl.multiple_of(8 * starts[2] + xl * u_span, LANES)
            tq = stage[yy, :, pl.ds(q_at, q_span)].T
            tu = stage[yy, :, pl.ds(u_at, u_span)].T
            for zz in range(4):
                to = ct_ref.at[yy * 4 + zz, part]
                n = rows_of[0]
                to[:n] = tq[zz * n : (zz + 1) * n]
                n = rows_of[1]
                k_at = pl.multiple_of(xl * 4 * n + zz * n, 16)
                to[starts[1] : starts[2]] = kt_buf[yy, pl.ds(k_at, n)]
                n = rows_of[2]
                to[starts[2] :] = tu[zz * n : (zz + 1) * n]
            return carry

        lax.fori_loop(0, 4, one, 0)

    own_x = fetch(x_ref, x_buf.at[pl.ds(0, LANES)])
    own_sends(0)
    along_z = {}
    for copy in staged:
        copy.wait()
    turn(0)
    c_sends(0)
    own_c = [fetch(ct_piece(0, 0, 0), c_block(0, 0))]
    turn(1)
    own_c.append(fetch(ct_piece(1, 0, 0), c_block(1, 0)))
    loaded = []
    for i, refs in enumerate(
        ((wq_ref, wk_ref, wu_ref), (mq_ref, mk_ref, mu_ref), (vq_ref, vk_ref, vu_ref))
    ):
        for ref, n, at in zip(refs, rows_of, starts):
            loaded.append(fetch(ref, opt_buf.at[i, pl.ds(at, n)]))

    def share(part, slot):
        at = c_block(part, slot)
        shared[part].append(go(remote(at, at, device(flip_core=True))))

    def pass_on(part, slot):
        at = c_block(part, slot)
        passed[part].append(go(remote(at, at, device(flip_lo=True))))

    def c_direct(part):
        shared[part] = []
        passed[part] = []
        own_c[part].wait()
        share(part, 0)
        for copy, dy in zip(near[part], (1, 3, 2)):
            copy.wait_recv()
            share(part, ((-dy) % 4) * 4)
        if part == 0:
            along_z[0] = z_sends(0)
        for copy, dy in zip(facing[part], order):
            copy.wait_recv()
            slot = wrap(-dy) * 4 + mine
            pass_on(part, slot)
            share(part, slot)
        for i, copy in enumerate(far[part]):
            copy.wait_recv()
            slot = wrap(-((1 - lo) + 2 * i)) * 4 + 2
            pass_on(part, slot)
            share(part, slot)

    def c_passed(part):
        for copy, dy in zip(passed[part][:4], order):
            copy.wait_recv()
            share(part, wrap(-dy) * 4 + side)
        for i, copy in enumerate(passed[part][4:]):
            copy.wait_recv()
            share(part, wrap(-(lo + 2 * i)) * 4 + 2)

    def c_ready(part):
        for copy in shared[part]:
            copy.wait_recv()

    up, down, fwd_up, fwd_down = {}, {}, {}, {}

    def stage_y(j):
        for copy in along_z[j]:
            copy.wait_recv()
        if j + 2 < CHUNKS:
            along_z[j + 2] = z_sends(j + 2)
        src = x_buf.at[pl.ds(LANES, 3 * LANES), cols(j)]
        up[j] = go(remote(src, x_buf.at[pl.ds(13 * LANES, 3 * LANES), cols(j)], device(dy=1)))
        down[j] = go(remote(src, x_buf.at[pl.ds(5 * LANES, 3 * LANES), cols(j)], device(dy=3)))

    def stage_forward(j):
        up[j].wait_recv()
        fwd_up[j] = go(
            remote(
                x_buf.at[pl.ds(13 * LANES, LANES), cols(j)],
                x_buf.at[pl.ds(9 * LANES, LANES), cols(j)],
                device(dy=1),
            )
        )
        down[j].wait_recv()
        fwd_down[j] = go(
            remote(
                x_buf.at[pl.ds(6 * LANES, 2 * LANES), cols(j)],
                x_buf.at[pl.ds(10 * LANES, 2 * LANES), cols(j)],
                device(dy=3),
            )
        )

    ring = {}

    def ring_send(j, step):
        for way, sign in ((0, 1), (1, -1)):
            target = wrap(x - sign * (step + 1))
            if step > 0:
                ring[j, step - 1, way].wait_recv()
                p_buf[j, target, way] = p_buf[j, target, way] + r_buf[j, step - 1, way]
            ring[j, step, way] = go(
                remote(p_buf.at[j, target, way], r_buf.at[j, step, way], device(dx=sign))
            )

    def finish(j):
        if j == 0:
            for copy in loaded:
                copy.wait()
            lane_power[...] = jnp.zeros_like(lane_power)
        for way in (0, 1):
            ring[j, 2, way].wait_recv()
            at = pl.ds(j * width + way * (width // 2), width // 2)
            gradient = p_buf[j, x, way] + r_buf[j, 2, way]
            weight = opt_buf[0, :, at].astype(jnp.float32)
            moment = opt_buf[1, :, at].astype(jnp.float32)
            second = opt_buf[2, :, at].astype(jnp.float32)
            first = beta_one * moment + (1.0 - beta_one) * gradient
            square = beta_two * second + (1.0 - beta_two) * gradient * gradient
            step = weight - rate * first / (jnp.sqrt(square) + eps_adam)
            mean_ref[:, at] = first.astype(jnp.bfloat16)
            square_ref[:, at] = square.astype(jnp.bfloat16)
            step_ref[:, at] = step
            lane_power[...] += step * step

    def gather_power():
        ones = jnp.ones((8, LANES), jnp.float32)
        power_in[0] = lax.dot_general(
            ones,
            lane_power[...],
            (((1,), (1,)), ((), ())),
            precision=lax.Precision.HIGHEST,
            preferred_element_type=jnp.float32,
        )
        copies = [
            go(remote(power_in.at[0], power_in.at[i], to))
            for i, to in (
                (1, device(flip_core=True)),
                (2, device(flip_lo=True)),
                (3, device(flip_lo=True, flip_core=True)),
            )
        ]
        for copy in copies:
            copy.wait_recv()
        pair = [power_in[0] + power_in[1], power_in[2] + power_in[3]]
        power_ref[...] = pair[0] + pair[1]

    def multiply(j, part):
        def one(i, carry):
            d = wrap(x + 1 + part + 2 * i)
            lhs = jnp.concatenate([c_buf[k, d] for k in range(16)], axis=1)
            out = jnp.dot(lhs, x_buf[:, cols(j)], preferred_element_type=jnp.float32)
            p_buf[j, d, 0] = out[:, : width // 2]
            p_buf[j, d, 1] = out[:, width // 2 :]
            return carry

        lax.fori_loop(0, 2, one, 0)

    def arrived(j):
        fwd_up[j].wait_recv()
        fwd_down[j].wait_recv()

    c_direct(0)
    c_sends(1)
    along_z[1] = z_sends(1)
    own_forward(0)
    stage_y(0)
    c_passed(0)
    c_ready(0)
    stage_forward(0)
    own_sends(1)
    stage_y(1)
    c_direct(1)
    own_x.wait()
    own_arrived(0)
    arrived(0)
    multiply(0, 0)
    ring_send(0, 0)
    stage_forward(1)
    c_passed(1)
    stage_y(2)
    own_forward(1)
    c_ready(1)
    multiply(0, 1)

    for j in range(1, CHUNKS + 4):
        if j == CHUNKS // 2:
            own_arrived(1)
        if j < CHUNKS:
            arrived(j)
            multiply(j, 0)
            ring_send(j, 0)
        if j + 1 < CHUNKS:
            stage_forward(j + 1)
        if j < CHUNKS:
            multiply(j, 1)
        if 0 <= j - 1 < CHUNKS:
            ring_send(j - 1, 1)
        if j + 2 < CHUNKS:
            stage_y(j + 2)
        if 0 <= j - 2 < CHUNKS:
            ring_send(j - 2, 2)
        if 0 <= j - 4 < CHUNKS:
            finish(j - 4)
    gather_power()
    for copy in pending:
        copy.wait_send()


def final_kernel(
    step_ref,
    mean_ref,
    square_ref,
    power_ref,
    new_q,
    new_k,
    new_u,
    mean_q,
    mean_k,
    mean_u,
    square_q,
    square_k,
    square_u,
):
    total = power_ref[...].T[:, :1]
    width = 4 * step_ref.shape[1]
    scale = 1.0 / jnp.sqrt(total / width + eps_norm)
    at = 0
    for new, mean, square in (
        (new_q, mean_q, square_q),
        (new_k, mean_k, square_k),
        (new_u, mean_u, square_u),
    ):
        rows = pl.ds(at, new.shape[0])
        part = scale[at : at + new.shape[0]]
        new[...] = (step_ref[rows, :] * part).astype(jnp.bfloat16)
        mean[...] = mean_ref[rows, :]
        square[...] = square_ref[rows, :]
        at += new.shape[0]


def per_device(*arguments):
    layer_input = arguments[0]
    weights = arguments[4:7]
    tokens, width = layer_input.shape
    rows = sum(w.shape[0] for w in weights)
    chunk = width // CHUNKS
    count = 2 * (9 + 6 + 16) + 6 + CHUNKS * (3 + 4 + 6) + 3
    vmem = pl.BlockSpec(memory_space=pltpu.VMEM)
    step, mean, square, power = pl.pallas_call(
        exchange_kernel,
        out_shape=(
            jax.ShapeDtypeStruct((rows, width), jnp.float32),
            jax.ShapeDtypeStruct((rows, width), jnp.bfloat16),
            jax.ShapeDtypeStruct((rows, width), jnp.bfloat16),
            jax.ShapeDtypeStruct((8, rows), jnp.float32),
        ),
        in_specs=[pl.BlockSpec(memory_space=pl.ANY)] * 13,
        out_specs=(vmem,) * 4,
        scratch_shapes=[
            pltpu.VMEM((4, tokens, 8 * rows), jnp.bfloat16),
            pltpu.VMEM((4, LANES, tokens), jnp.bfloat16),
            pltpu.VMEM((16, 2, rows, tokens), jnp.bfloat16),
            pltpu.VMEM((3, rows, width), jnp.bfloat16),
            pltpu.VMEM((16, 4, rows, tokens), jnp.bfloat16),
            pltpu.VMEM((16 * tokens, width), jnp.bfloat16),
            pltpu.VMEM((CHUNKS, 4, 2, rows, chunk // 2), jnp.float32),
            pltpu.VMEM((CHUNKS, 3, 2, rows, chunk // 2), jnp.float32),
            pltpu.VMEM((rows, LANES), jnp.float32),
            pltpu.VMEM((4, 8, rows), jnp.float32),
            pltpu.SemaphoreType.DMA((count,)),
            pltpu.SemaphoreType.DMA((count,)),
            pltpu.SemaphoreType.DMA((12 + 1 + 2 + 9,)),
        ],
        compiler_params=pltpu.CompilerParams(
            collective_id=0, has_side_effects=True, vmem_limit_bytes=60 << 20
        ),
        name="exchange",
    )(*arguments)
    shapes = tuple(jax.ShapeDtypeStruct(w.shape, jnp.bfloat16) for w in weights)
    return pl.pallas_call(
        final_kernel,
        out_shape=shapes * 3,
        in_specs=[vmem] * 4,
        out_specs=(vmem,) * 9,
        compiler_params=pltpu.CompilerParams(vmem_limit_bytes=40 << 20),
        name="final",
    )(step, mean, square, power)


def solution(mesh):
    spread = P("dp", "col")
    return jax.shard_map(
        per_device,
        mesh=mesh,
        in_specs=(spread,) + (P("dp", None),) * 3 + (spread,) * 9,
        out_specs=(spread,) * 9,
        check_vma=False,
    )
```

```python
import functools

import jax
import jax.numpy as jnp
from jax import lax
from jax.experimental import pallas as pl
from jax.experimental.pallas import tpu as pltpu
from jax.sharding import PartitionSpec as P

beta_one = 0.9
beta_two = 0.95
rate = 0.1
eps_adam = 1e-08
eps_norm = 1e-06

MESH = pl.DeviceIdType.MESH
LANES = 128
WIDTHS = (256,) * 8
STARTS = tuple(sum(WIDTHS[:j]) for j in range(len(WIDTHS)))
CHUNKS = len(WIDTHS)


def place():
    dp = lax.axis_index("dp")
    col = lax.axis_index("col")
    return dp // 16, lax.rem(dp // 4, 4), lax.rem(dp, 4), col // 2, lax.rem(col, 2)


def wrap(v):
    return lax.rem(v + 8, 4)


def exchange_kernel(
    x_ref,
    q_ref,
    k_ref,
    u_ref,
    wq_ref,
    wk_ref,
    wu_ref,
    mq_ref,
    mk_ref,
    mu_ref,
    vq_ref,
    vk_ref,
    vu_ref,
    step_ref,
    mean_ref,
    square_ref,
    power_ref,
    stage,
    kt_buf,
    ct_ref,
    opt_buf,
    c_buf,
    x_buf,
    p_buf,
    r_buf,
    lane_power,
    power_in,
    ssem,
    rsem,
    lsem,
):
    y, x, z, lo, core = place()
    rows_of = (wq_ref.shape[0], wk_ref.shape[0], wu_ref.shape[0])
    starts = (0, rows_of[0], rows_of[0] + rows_of[1])
    local = []

    def fetch(src, dst):
        copy = pltpu.make_async_copy(src, dst, lsem.at[len(local)])
        local.append(copy)
        copy.start()
        return copy

    staged = []
    for yy in range(4):
        for ref, n, at in zip((q_ref, k_ref, u_ref), rows_of, starts):
            span = 8 * n
            src = ref.at[:, pl.ds(pl.multiple_of((2 * yy + core) * span, LANES), span)]
            staged.append(fetch(src, stage.at[yy, :, pl.ds(8 * at, span)]))
    toward = 2 * lo - 1
    rows = step_ref.shape[0]

    def device(dy=0, dx=0, dz=0, flip_lo=False, flip_core=False):
        lo_to = 1 - lo if flip_lo else lo
        core_to = 1 - core if flip_core else core
        return {
            "dp": wrap(y + dy) * 16 + wrap(x + dx) * 4 + wrap(z + dz),
            "col": lo_to * 2 + core_to,
        }

    peers = [device(dy=d) for d in (1, 2, 3)]
    peers += [device(dz=d) for d in (1, 2, 3)]
    peers += [device(dx=d) for d in (1, 3)]
    peers += [device(dy=d, dz=toward, flip_lo=True) for d in range(4)]
    peers += [device(dy=d, dz=2, flip_lo=True) for d in range(4)]
    peers += [device(flip_lo=True), device(flip_core=True)]
    peers += [device(flip_lo=True, flip_core=True)]
    barrier = pltpu.get_barrier_semaphore()
    for peer in peers:
        pl.semaphore_signal(barrier, inc=1, device_id=peer, device_id_type=MESH)
    pl.semaphore_wait(barrier, len(peers))

    used = [0]
    pending = []

    def remote(src, dst, to):
        k = used[0]
        used[0] += 1
        return pltpu.make_async_remote_copy(
            src_ref=src,
            dst_ref=dst,
            send_sem=ssem.at[k],
            recv_sem=rsem.at[k],
            device_id=to,
            device_id_type=MESH,
        )

    def go(copy):
        copy.start()
        pending.append(copy)
        return copy

    odd = lax.rem(x, 2)
    inner = (1 - odd, odd)

    def c_block(part, slot):
        return c_buf.at[slot, 2 * core + inner[part]]

    def ct_piece(part, dy, dz):
        return ct_ref.at[wrap(y + dy) * 4 + wrap(z + dz), part]

    def send_c(part, slot, dy, dz, flip):
        to = device(dy=dy, dz=dz, flip_lo=flip)
        return go(remote(ct_piece(part, dy, dz), c_block(part, slot), to))

    def cols(j):
        return pl.ds(STARTS[j], WIDTHS[j])

    order = (0, 1, 3, 2)
    side = wrap(-toward)
    mine = wrap(toward)
    facing, far, near, passed, shared = {}, {}, {}, {}, {}

    def c_sends(part):
        facing[part] = [
            send_c(part, wrap(-dy) * 4 + side, dy, toward, True) for dy in order
        ]
        far[part] = [
            send_c(part, wrap(-(lo + 2 * i)) * 4 + 2, lo + 2 * i, 2, True) for i in range(2)
        ]
        near[part] = [send_c(part, ((-dy) % 4) * 4, dy, 0, False) for dy in (1, 3, 2)]

    def z_sends(j):
        return [
            go(
                remote(
                    x_ref.at[:, cols(j)],
                    x_buf.at[pl.ds(((-dz) % 4) * LANES, LANES), cols(j)],
                    device(dz=dz),
                )
            )
            for dz in (1, 3, 2)
        ]

    own_up, own_down, own_fwd = {}, {}, {}

    def halves(h):
        return pl.ds(h * (x_ref.shape[1] // 2), x_ref.shape[1] // 2)

    def own_sends(h):
        at = halves(h)
        src = x_ref.at[:, at]
        own_up[h] = go(remote(src, x_buf.at[pl.ds(12 * LANES, LANES), at], device(dy=1)))
        own_down[h] = go(remote(src, x_buf.at[pl.ds(4 * LANES, LANES), at], device(dy=3)))

    def own_forward(h):
        own_up[h].wait_recv()
        src = x_buf.at[pl.ds(12 * LANES, LANES), halves(h)]
        own_fwd[h] = go(
            remote(src, x_buf.at[pl.ds(8 * LANES, LANES), halves(h)], device(dy=1))
        )

    def own_arrived(h):
        own_down[h].wait_recv()
        own_fwd[h].wait_recv()

    def turn(part):
        xl = inner[part]

        def one(yy, carry):
            if part == 0:
                kt_buf[yy] = stage[yy, :, 8 * starts[1] : 8 * starts[2]].T
            q_span, u_span = 4 * rows_of[0], 4 * rows_of[2]
            q_at = pl.multiple_of(xl * q_span, LANES)
            u_at = pl.multiple_of(8 * starts[2] + xl * u_span, LANES)
            tq = stage[yy, :, pl.ds(q_at, q_span)].T
            tu = stage[yy, :, pl.ds(u_at, u_span)].T
            for zz in range(4):
                to = ct_ref.at[yy * 4 + zz, part]
                n = rows_of[0]
                to[:n] = tq[zz * n : (zz + 1) * n]
                n = rows_of[1]
                k_at = pl.multiple_of(xl * 4 * n + zz * n, 16)
                to[starts[1] : starts[2]] = kt_buf[yy, pl.ds(k_at, n)]
                n = rows_of[2]
                to[starts[2] :] = tu[zz * n : (zz + 1) * n]
            return carry

        lax.fori_loop(0, 4, one, 0)

    up, down, fwd_up, fwd_down = {}, {}, {}, {}

    def stage_y(j):
        for copy in along_z[j]:
            copy.wait_recv()
        src = x_buf.at[pl.ds(LANES, 3 * LANES), cols(j)]
        up[j] = go(remote(src, x_buf.at[pl.ds(13 * LANES, 3 * LANES), cols(j)], device(dy=1)))
        down[j] = go(remote(src, x_buf.at[pl.ds(5 * LANES, 3 * LANES), cols(j)], device(dy=3)))

    def stage_forward(j):
        up[j].wait_recv()
        fwd_up[j] = go(
            remote(
                x_buf.at[pl.ds(13 * LANES, LANES), cols(j)],
                x_buf.at[pl.ds(9 * LANES, LANES), cols(j)],
                device(dy=1),
            )
        )
        down[j].wait_recv()
        fwd_down[j] = go(
            remote(
                x_buf.at[pl.ds(6 * LANES, 2 * LANES), cols(j)],
                x_buf.at[pl.ds(10 * LANES, 2 * LANES), cols(j)],
                device(dy=3),
            )
        )

    own_x = fetch(x_ref, x_buf.at[pl.ds(0, LANES)])
    own_sends(0)
    along_z = {0: z_sends(0)}
    for copy in staged:
        copy.wait()
    turn(0)
    c_sends(0)
    own_c = [fetch(ct_piece(0, 0, 0), c_block(0, 0))]
    stage_y(0)
    own_forward(0)
    own_sends(1)
    turn(1)
    own_c.append(fetch(ct_piece(1, 0, 0), c_block(1, 0)))
    loaded = []
    for i, refs in enumerate(
        ((wq_ref, wk_ref, wu_ref), (mq_ref, mk_ref, mu_ref), (vq_ref, vk_ref, vu_ref))
    ):
        for ref, n, at in zip(refs, rows_of, starts):
            loaded.append(fetch(ref, opt_buf.at[i, pl.ds(at, n)]))

    def share(part, slot):
        at = c_block(part, slot)
        shared[part].append(go(remote(at, at, device(flip_core=True))))

    def pass_on(part, slot):
        at = c_block(part, slot)
        passed[part].append(go(remote(at, at, device(flip_lo=True))))

    def c_direct(part, after_near, after_facing, after_far):
        shared[part] = []
        passed[part] = []
        own_c[part].wait()
        share(part, 0)
        for copy, dy in zip(near[part], (1, 3, 2)):
            copy.wait_recv()
            share(part, ((-dy) % 4) * 4)
        after_near()
        for copy, dy in zip(facing[part], order):
            copy.wait_recv()
            slot = wrap(-dy) * 4 + mine
            pass_on(part, slot)
            share(part, slot)
        after_facing()
        for i, copy in enumerate(far[part]):
            copy.wait_recv()
            slot = wrap(-((1 - lo) + 2 * i)) * 4 + 2
            pass_on(part, slot)
            share(part, slot)
        after_far()

    def z_issue(j):
        along_z[j] = z_sends(j)

    def c_passed(part):
        for copy, dy in zip(passed[part][:4], order):
            copy.wait_recv()
            share(part, wrap(-dy) * 4 + side)
        for i, copy in enumerate(passed[part][4:]):
            copy.wait_recv()
            share(part, wrap(-(lo + 2 * i)) * 4 + 2)

    def c_ready(part):
        for copy in shared[part]:
            copy.wait_recv()

    ring = {}

    def rows_way(way):
        return pl.ds(way * (rows // 2), rows // 2)

    def ring_send(j, step):
        for way, sign in ((0, 1), (1, -1)):
            target = wrap(x - sign * (step + 1))
            at = (rows_way(way), cols(j))
            if step > 0:
                ring[j, step - 1, way].wait_recv()
                p_buf[(target,) + at] = p_buf[(target,) + at] + r_buf[(step - 1,) + at]
            ring[j, step, way] = go(
                remote(p_buf.at[(target,) + at], r_buf.at[(step,) + at], device(dx=sign))
            )

    def finish(j):
        if j == 0:
            for copy in loaded:
                copy.wait()
            lane_power[...] = jnp.zeros_like(lane_power)
        for way in (0, 1):
            ring[j, 2, way].wait_recv()
        for lane in range(STARTS[j], STARTS[j] + WIDTHS[j], LANES):
            at = pl.ds(lane, LANES)
            gradient = p_buf[x, :, at] + r_buf[2, :, at]
            weight = opt_buf[0, :, at].astype(jnp.float32)
            moment = opt_buf[1, :, at].astype(jnp.float32)
            second = opt_buf[2, :, at].astype(jnp.float32)
            first = beta_one * moment + (1.0 - beta_one) * gradient
            square = beta_two * second + (1.0 - beta_two) * gradient * gradient
            step = weight - rate * first / (jnp.sqrt(square) + eps_adam)
            mean_ref[:, at] = first.astype(jnp.bfloat16)
            square_ref[:, at] = square.astype(jnp.bfloat16)
            step_ref[:, at] = step
            lane_power[...] += step * step

    def gather_power():
        ones = jnp.ones((8, LANES), jnp.float32)
        power_in[0] = lax.dot_general(
            ones,
            lane_power[...],
            (((1,), (1,)), ((), ())),
            precision=lax.Precision.HIGHEST,
            preferred_element_type=jnp.float32,
        )
        copies = [
            go(remote(power_in.at[0], power_in.at[i], to))
            for i, to in (
                (1, device(flip_core=True)),
                (2, device(flip_lo=True)),
                (3, device(flip_lo=True, flip_core=True)),
            )
        ]
        for copy in copies:
            copy.wait_recv()
        pair = [power_in[0] + power_in[1], power_in[2] + power_in[3]]
        power_ref[...] = pair[0] + pair[1]

    def multiply(j, part):
        def one(i, carry):
            d = wrap(x + 1 + part + 2 * i)
            lhs = jnp.concatenate([c_buf[k, d] for k in range(16)], axis=1)
            out = jnp.dot(lhs, x_buf[:, cols(j)], preferred_element_type=jnp.float32)
            p_buf[d, :, cols(j)] = out
            return carry

        lax.fori_loop(0, 2, one, 0)

    def arrived(j):
        fwd_up[j].wait_recv()
        fwd_down[j].wait_recv()

    def early():
        z_issue(1)
        stage_forward(0)

    c_direct(0, early, lambda: None, lambda: c_sends(1))
    stage_y(1)
    c_passed(0)
    own_forward(1)
    c_ready(0)
    own_x.wait()
    own_arrived(0)
    arrived(0)
    multiply(0, 0)
    ring_send(0, 0)
    c_direct(1, lambda: z_issue(2), lambda: stage_forward(1), lambda: z_issue(3))
    stage_y(2)
    arrived(1)
    multiply(1, 0)
    ring_send(1, 0)
    c_passed(1)
    z_issue(4)
    c_ready(1)
    multiply(0, 1)
    ring_send(0, 1)
    stage_y(3)
    z_issue(5)
    stage_forward(2)
    multiply(1, 1)
    ring_send(1, 1)

    ys, zs = 4, 6
    half_at = min(j for j in range(CHUNKS) if STARTS[j] + WIDTHS[j] > x_ref.shape[1] // 2)
    for j in range(2, CHUNKS + 4):
        if j == half_at:
            own_arrived(1)
        if j < CHUNKS:
            arrived(j)
            multiply(j, 0)
            ring_send(j, 0)
        while ys < min(j + 3, CHUNKS):
            stage_y(ys)
            ys += 1
            if zs < CHUNKS:
                z_issue(zs)
                zs += 1
        if j + 1 < CHUNKS:
            stage_forward(j + 1)
        if j < CHUNKS:
            multiply(j, 1)
        if 2 <= j - 1 < CHUNKS:
            ring_send(j - 1, 1)
        if 0 <= j - 2 < CHUNKS:
            ring_send(j - 2, 2)
        if 0 <= j - 4 < CHUNKS:
            finish(j - 4)
    gather_power()
    for copy in pending:
        copy.wait_send()


def final_kernel(*refs):
    step_ref, mean_ref, square_ref, power_ref = refs[:4]
    outputs = refs[4:13]
    step_buf, mean_buf, square_buf, power_buf, new_buf, sems = refs[13:]
    started = []

    def move(src, dst):
        copy = pltpu.make_async_copy(src, dst, sems.at[len(started)])
        started.append(copy)
        copy.start()
        return copy

    def spread(buf, targets):
        at = 0
        for target in targets:
            rows = target.shape[0]
            leaving.append(move(buf.at[pl.ds(at, rows)], target))
            at += rows

    leaving = []
    power = move(power_ref, power_buf)
    step = move(step_ref, step_buf)
    mean = move(mean_ref, mean_buf)
    square = move(square_ref, square_buf)
    power.wait()
    total = power_buf[...].T[:, :1]
    scale = 1.0 / jnp.sqrt(total / (4 * step_buf.shape[1]) + eps_norm)
    step.wait()
    new_buf[...] = (step_buf[...] * scale).astype(jnp.bfloat16)
    mean.wait()
    spread(mean_buf, outputs[3:6])
    square.wait()
    spread(square_buf, outputs[6:9])
    spread(new_buf, outputs[0:3])
    for copy in leaving:
        copy.wait()


def per_device(*arguments):
    layer_input = arguments[0]
    weights = arguments[4:7]
    tokens, width = layer_input.shape
    rows = sum(w.shape[0] for w in weights)
    count = 2 * (9 + 6 + 16) + 6 + CHUNKS * (3 + 4 + 6) + 3
    vmem = pl.BlockSpec(memory_space=pltpu.VMEM)
    hbm = pl.BlockSpec(memory_space=pl.ANY)
    step, mean, square, power = pl.pallas_call(
        exchange_kernel,
        out_shape=(
            jax.ShapeDtypeStruct((rows, width), jnp.float32),
            jax.ShapeDtypeStruct((rows, width), jnp.bfloat16),
            jax.ShapeDtypeStruct((rows, width), jnp.bfloat16),
            jax.ShapeDtypeStruct((8, rows), jnp.float32),
        ),
        in_specs=[pl.BlockSpec(memory_space=pl.ANY)] * 13,
        out_specs=(vmem,) * 4,
        scratch_shapes=[
            pltpu.VMEM((4, tokens, 8 * rows), jnp.bfloat16),
            pltpu.VMEM((4, LANES, tokens), jnp.bfloat16),
            pltpu.VMEM((16, 2, rows, tokens), jnp.bfloat16),
            pltpu.VMEM((3, rows, width), jnp.bfloat16),
            pltpu.VMEM((16, 4, rows, tokens), jnp.bfloat16),
            pltpu.VMEM((16 * tokens, width), jnp.bfloat16),
            pltpu.VMEM((4, rows, width), jnp.float32),
            pltpu.VMEM((3, rows, width), jnp.float32),
            pltpu.VMEM((rows, LANES), jnp.float32),
            pltpu.VMEM((4, 8, rows), jnp.float32),
            pltpu.SemaphoreType.DMA((count,)),
            pltpu.SemaphoreType.DMA((count,)),
            pltpu.SemaphoreType.DMA((12 + 1 + 2 + 9,)),
        ],
        compiler_params=pltpu.CompilerParams(
            collective_id=0, has_side_effects=True, vmem_limit_bytes=60 << 20
        ),
        name="exchange",
    )(*arguments)
    shapes = tuple(jax.ShapeDtypeStruct(w.shape, jnp.bfloat16) for w in weights)
    return pl.pallas_call(
        final_kernel,
        out_shape=shapes * 3,
        in_specs=[hbm] * 4,
        out_specs=(hbm,) * 9,
        scratch_shapes=[
            pltpu.VMEM((rows, width), jnp.float32),
            pltpu.VMEM((rows, width), jnp.bfloat16),
            pltpu.VMEM((rows, width), jnp.bfloat16),
            pltpu.VMEM((8, rows), jnp.float32),
            pltpu.VMEM((rows, width), jnp.bfloat16),
            pltpu.SemaphoreType.DMA((13,)),
        ],
        compiler_params=pltpu.CompilerParams(vmem_limit_bytes=60 << 20),
        name="final",
    )(step, mean, square, power)


def solution(mesh):
    spread = P("dp", "col")
    return jax.shard_map(
        per_device,
        mesh=mesh,
        in_specs=(spread,) + (P("dp", None),) * 3 + (spread,) * 9,
        out_specs=(spread,) * 9,
        check_vma=False,
    )
```
